32 devices in a mesh: tm: 4 (over x, core), cohort: 8 (over z, y).
Axes of the slice: x: 2, y: 2, z: 4, core: 2. Of those that a mesh axis runs over, the one named last changes fastest.
Arguments:
- transition: float32 [32, 16, 256, 256], P('tm', 'cohort'), may hold values from 0 to 1, as said below
- entry: int32 [16], P('cohort'), may hold values from 0 to 31, as said below
- share: float32 [16], P('cohort'), may hold values from 0.1 to 1
Outputs:
- cumulative: float32 [32, 16, 256, 256], P('tm', 'cohort')
- pooled: float32 [32, 256, 256], P('tm', 'cohort')
The draws below stay inside these ranges and needn't reach their ends.
Inputs may be any that keep to these rules, and one draw needn't show every extreme that they name: `entry`: month numbers within the window; some group enters at month 0 and some at the window's last month. `transition`: each row of every monthly matrix is nonnegative and sums to one, with a diagonal entry of at least 0.7.
All inputs are finite; a program needn't handle non-finite values.
Results may differ from the reference program's by a relative error of at most 0.0001.
Values sent between devices are 32-bit elements; how exact they have to be, the bound alone decides.
No kernel may reach another device: no remote copies, remote signals or barrier semaphores. Data moves between devices by JAX's collectives and lax.ppermute only.
A program may use at most 64 MiB of HBM per device.

```python
import math
import jax
import jax.numpy as jnp
from jax import lax

NS = 256
MONTHS = 32
GROUPS = 16


def draw_transition(key, part):
    keys = jax.random.split(jax.random.fold_in(key, 11), 4)
    diag_low, diag_high, widest, power, far_power, far_share = (0.7, 0.8, 8, 1.0, 24.0, 0.5)
    diag_part = jax.random.uniform(keys[0], (MONTHS, GROUPS, NS, 1), jnp.float32, diag_low, diag_high)
    reach = jax.random.randint(keys[1], (MONTHS, GROUPS, NS, 1), 1, widest + 1)
    row_index = jnp.arange(NS)[:, None]
    column_index = jnp.arange(NS)[None, :]
    distance = jnp.abs(row_index - column_index)
    in_band = (distance >= 1) & (distance <= reach)
    raw_band = jax.random.uniform(keys[2], (MONTHS, GROUPS, NS, NS), jnp.float32, 0.0, 1.0) ** power + 0.001
    band = jnp.where(in_band, raw_band, 0.0)
    band = band / jnp.sum(band, axis=-1, keepdims=True)
    unit = jnp.eye(NS, dtype=jnp.float32)
    raw_far = jax.random.uniform(keys[3], (MONTHS, GROUPS, NS, NS), jnp.float32, 0.0, 1.0) ** far_power + 0.001
    far_part = raw_far * (1.0 - unit)
    far_part = far_part / jnp.sum(far_part, axis=-1, keepdims=True)
    off_part = (1.0 - diag_part) * ((1.0 - far_share) * band + far_share * far_part)
    return (off_part + diag_part * unit).astype(jnp.float32)


def draw_entry(key, part):
    base_key, pick_key = jax.random.split(jax.random.fold_in(key, 23))
    values = jax.random.randint(base_key, (GROUPS,), 0, MONTHS)
    picks = jax.random.permutation(pick_key, GROUPS)
    values = values.at[picks[0]].set(0)
    values = values.at[picks[1]].set(MONTHS - 1)
    return values.astype(jnp.int32)


def shard_levels(stream_key, dims, shards, low, top_value):
    loudness = 1.0
    for axis_at, shards_of in shards:
        draws = jax.random.uniform(jax.random.fold_in(jax.random.fold_in(stream_key, 6), axis_at), (shards_of,), jnp.float32, low / len(shards), top_value / len(shards))
        loudness = loudness * jnp.repeat(jnp.exp(draws), dims[axis_at] // shards_of).reshape((-1,) + (1,) * (len(dims) - 1 - axis_at))
    return loudness


def setup_inputs(seed: int = 0) -> dict:
    streams_of = jax.random.split(jax.random.key(seed), 4)
    return {
        "transition": draw_transition(jax.random.fold_in(streams_of[3], 71), 0),
        "entry": draw_entry(jax.random.fold_in(streams_of[3], 71), 0),
        "share": jnp.clip(jnp.exp(math.log(1.0) - 2.3025851 * jax.random.uniform(streams_of[2], (GROUPS,), jnp.float32) ** shard_levels(streams_of[2], (GROUPS,), ((0, 8),), -0.2, 0.2)), 0.1, 1.0),
    }


kernel_weights = (1.0 / 16, 2.0 / 16, 3.0 / 16, 4.0 / 16, 3.0 / 16, 2.0 / 16, 1.0 / 16)


def reference(transition, entry, share):
    months_all = transition.shape[0]
    states = transition.shape[2]
    padded = jnp.pad(transition, ((3, 3), (0, 0), (0, 0), (0, 0)))
    month_idx = jnp.arange(months_all).astype(jnp.int32)
    smoothed = jnp.zeros_like(transition)
    weight_sum = jnp.zeros((months_all,), transition.dtype)
    for offset in range(7):
        smoothed = smoothed + kernel_weights[offset] * padded[offset:offset + months_all]
        inside = (month_idx + offset - 3 >= 0) & (month_idx + offset - 3 < months_all)
        weight_sum = weight_sum + jnp.where(inside, kernel_weights[offset], 0.0).astype(transition.dtype)
    graduated = smoothed / weight_sum[:, None, None, None]
    unit = jnp.eye(states, dtype=transition.dtype)
    active = month_idx[:, None] >= entry[None, :]
    monthly = jnp.where(active[:, :, None, None], graduated, unit)

    def advance(running, matrix):
        nxt = jnp.einsum("gij,gjk->gik", running, matrix, precision=lax.Precision.HIGHEST)
        summed = jnp.einsum("g,gij->ij", share, nxt, precision=lax.Precision.HIGHEST)
        return nxt, (nxt, summed)

    start_state = jnp.broadcast_to(unit, transition.shape[1:])
    _, (cumulative, pooled) = lax.scan(advance, start_state, monthly)
    return cumulative, pooled
```

```python
import functools

import jax
import jax.numpy as jnp
from jax import lax
from jax.experimental import pallas as pl
from jax.experimental.pallas import tpu as pltpu
from jax.sharding import PartitionSpec as P

kernel_weights = (1.0 / 16, 2.0 / 16, 3.0 / 16, 4.0 / 16, 3.0 / 16, 2.0 / 16, 1.0 / 16)
REACH = 3
VMEM = pl.BlockSpec(memory_space=pltpu.VMEM)
SMEM = pl.BlockSpec(memory_space=pltpu.SMEM)
f32, bf16 = jnp.float32, jnp.bfloat16


def split(x):
    hi = x.astype(bf16)
    return hi, (x - hi.astype(f32)).astype(bf16)


def join(pair):
    return pair[0].astype(f32) + pair[1].astype(f32)


def product(a, b):
    dot = functools.partial(jnp.dot, preferred_element_type=f32)
    return dot(a[0], b[0]) + (dot(a[0], b[1]) + dot(a[1], b[0]))


def params(mib):
    return pltpu.CompilerParams(vmem_limit_bytes=mib << 20)


def cost(flops, touched):
    return pl.CostEstimate(flops=flops, bytes_accessed=touched, transcendentals=0)


def own_sums(months, raw_ref, sums_ref):
    for month in range(months):
        taps = [
            kernel_weights[offset + REACH] * raw_ref[month + offset]
            for offset in range(-REACH, REACH + 1)
            if 0 <= month + offset < months
        ]
        sums_ref[month] = sum(taps[1:], taps[0])


def own_sums_kernel(raw_ref, sums_ref):
    months, groups, states = raw_ref.shape[:3]

    @pl.loop(0, groups)
    def _(group):
        @pl.loop(0, states // 32)
        def _(chunk):
            rows = pl.ds(pl.multiple_of(chunk * 32, 32), 32)
            own_sums(months, raw_ref.at[:, group, rows], sums_ref.at[:, group, rows])


def inverse_weight(month, months_all):
    value = jnp.float32(1.0)
    for edge in range(months_all):
        inside = [
            kernel_weights[k + REACH]
            for k in range(-REACH, REACH + 1)
            if 0 <= edge + k < months_all
        ]
        if len(inside) < len(kernel_weights):
            value = jnp.where(month == edge, jnp.float32(1.0 / sum(inside)), value)
    return value


def tree(parts):
    while len(parts) > 1:
        nxt = [split(product(a, b)) for a, b in zip(parts[::2], parts[1::2])]
        parts = nxt + parts[len(nxt) * 2 :]
    return parts[0]


def months_kernel(months_all, sums_ref, low_ref, high_ref, entry_ref, hi_ref, lo_ref, total_ref):
    months, groups, states = sums_ref.shape[:3]
    first = lax.axis_index("tm") * months

    @pl.loop(0, groups)
    def _(group):
        @pl.loop(0, states // 32)
        def _(chunk):
            start = pl.multiple_of(chunk * 32, 32)
            rows = pl.ds(start, 32)
            shape = (32, states)
            row = lax.broadcasted_iota(jnp.int32, shape, 0) + start
            unit = (row == lax.broadcasted_iota(jnp.int32, shape, 1)).astype(f32)
            for month in range(months):
                value = sums_ref[month, group, rows]
                for offset in range(-REACH, REACH + 1):
                    weight = kernel_weights[offset + REACH]
                    if month + offset < 0:
                        value = value + weight * low_ref[month + offset + REACH, group, rows]
                    if month + offset >= months:
                        value = value + weight * high_ref[month + offset - months, group, rows]
                value = value * inverse_weight(first + month, months_all)
                value = jnp.where(first + month >= entry_ref[group], value, unit)
                hi, lo = split(value)
                hi_ref[month, group, rows] = hi
                lo_ref[month, group, rows] = lo

    parts = [
        [(hi_ref[month, group], lo_ref[month, group]) for month in range(months)]
        for group in range(groups)
    ]
    while len(parts[0]) > 2:
        parts = [
            [split(product(a, b)) for a, b in zip(p[::2], p[1::2])] + p[len(p) // 2 * 2 :]
            for p in parts
        ]
    for group in range(groups):
        total_ref[group] = product(*parts[group]) if len(parts[group]) > 1 else join(parts[group][0])


def pair_kernel(before_ref, total_ref, out_ref):
    for group in range(total_ref.shape[0]):
        out_ref[group] = product(split(before_ref[group]), split(total_ref[group]))


def prefix_kernel(hi_ref, lo_ref, before_ref, out_hi_ref, out_lo_ref):
    months, groups, states = hi_ref.shape[:3]
    second = lax.axis_index("tm") % 2 == 1
    shape = (states, states)
    row = lax.broadcasted_iota(jnp.int32, shape, 0)
    unit = (row == lax.broadcasted_iota(jnp.int32, shape, 1)).astype(f32)
    for group in range(groups):
        hi, lo = split(jnp.where(second, before_ref[group], unit))
        out_hi_ref[0, group] = hi
        out_lo_ref[0, group] = lo

    @pl.loop(0, months)
    def _(month):
        last = jnp.maximum(month - 1, 0)
        for group in range(groups):
            state = (out_hi_ref[last, group], out_lo_ref[last, group])
            hi, lo = split(product(state, (hi_ref[month, group], lo_ref[month, group])))
            out_hi_ref[month, group] = hi
            out_lo_ref[month, group] = lo


def apply_kernel(orders, hi_ref, lo_ref, carry_ref, share_ref, cum_ref, keep_ref, send_ref, mix_ref):
    groups, states = hi_ref.shape[1:3]
    chip = lax.axis_index("tm") // 2
    parity = lax.axis_index("tm") % 2
    me = lax.axis_index("cohort")
    rows = keep_ref.shape[2]
    half = keep_ref.shape[0]
    shape = (states, states)
    row = lax.broadcasted_iota(jnp.int32, shape, 0)
    unit = (row == lax.broadcasted_iota(jnp.int32, shape, 1)).astype(f32)
    mixed = jnp.zeros(shape, f32)
    for group in range(groups):
        carry = split(jnp.where(chip > 0, carry_ref[group], unit))
        value = product(carry, (hi_ref[0, group], lo_ref[0, group]))
        cum_ref[0, group] = value
        mixed = mixed + share_ref[group] * value
    mix_ref[...] = mixed
    for place in range(2 * half):
        away = jnp.where(parity == 0, place_of(orders[0], place), place_of(orders[1], place))
        start = pl.multiple_of((me ^ away) * rows, 8)
        out = keep_ref if place < half else send_ref
        out[place % half, 0] = mix_ref[pl.ds(start, rows), :]


def place_of(order, place):
    steps = len(order)
    return sum(order[s] for s in range(steps) if place >> (steps - 1 - s) & 1)


def halving_orders(count):
    bits = [1 << s for s in range(count.bit_length() - 1)]
    other = bits[:]
    if len(bits) > 1:
        other[0], other[1] = other[1], other[0]
    return bits, other


def on_device(mesh, transition, entry, share):
    months, groups, states = transition.shape[:3]
    lines, cohorts = mesh.shape["tm"], mesh.shape["cohort"]
    months_all = months * lines
    block = (states, states)
    shape = jax.ShapeDtypeStruct
    square = states**3
    size = transition.size * 4

    forward = [(i, i + 1) for i in range(lines - 1)]
    backward = [(b, a) for a, b in forward]
    low = lax.ppermute(transition[-REACH:], "tm", forward)
    high = lax.ppermute(transition[:REACH], "tm", backward)

    sums = pl.pallas_call(
        own_sums_kernel,
        out_shape=shape(transition.shape, f32),
        in_specs=[VMEM],
        out_specs=VMEM,
        compiler_params=params(16),
        cost_estimate=cost(13 * transition.size, 2 * size),
        name="own_sums",
    )(transition)
    hi, lo, total = pl.pallas_call(
        functools.partial(months_kernel, months_all),
        out_shape=(
            shape(transition.shape, bf16),
            shape(transition.shape, bf16),
            shape((groups,) + block, f32),
        ),
        in_specs=[VMEM, VMEM, VMEM, SMEM],
        out_specs=(VMEM, VMEM, VMEM),
        compiler_params=params(24),
        cost_estimate=cost(6 * months * groups * square, 3 * size),
        name="months",
    )(sums, low, high, entry)

    before = lax.ppermute(total, "tm", [(i, i + 1) for i in range(0, lines - 1, 2)])
    pair = pl.pallas_call(
        pair_kernel,
        out_shape=shape((groups,) + block, f32),
        in_specs=[VMEM, VMEM],
        out_specs=VMEM,
        compiler_params=params(16),
        cost_estimate=cost(6 * groups * square, 3 * groups * states * states * 4),
        name="pair",
    )(before, total)
    chip = lax.axis_index("tm") // 2
    carry = None
    for hop in range(1, lines // 2):
        if hop > 1:
            pair = pl.pallas_call(
                pair_kernel,
                out_shape=shape((groups,) + block, f32),
                in_specs=[VMEM, VMEM],
                out_specs=VMEM,
                compiler_params=params(16),
                name=f"pair{hop}",
            )(carry, first_pair)
        else:
            first_pair = pair
        at = 2 * hop
        to_first = lax.ppermute(pair, "tm", [(at - 1, at)])
        to_second = lax.ppermute(to_first, "tm", [(at, at + 1)])
        place = lax.axis_index("tm")
        arrived = jnp.where(place % 2 == 0, to_first, to_second)
        carry = arrived if carry is None else jnp.where(chip == hop, arrived, carry)
    if carry is None:
        carry = jnp.zeros_like(total)

    out_hi, out_lo = pl.pallas_call(
        prefix_kernel,
        out_shape=(shape(transition.shape, bf16), shape(transition.shape, bf16)),
        in_specs=[VMEM, VMEM, VMEM],
        out_specs=(VMEM, VMEM),
        compiler_params=params(24),
        cost_estimate=cost(6 * months * groups * square, 2 * size),
        name="prefix",
    )(hi, lo, before)

    orders = halving_orders(cohorts)
    steps = len(orders[0])
    rows = states // cohorts
    part = (cohorts // 2, 1, rows, states)
    by_month = lambda month: (month, 0, 0, 0)
    in_place = lambda month: (0, month, 0, 0)
    whole = lambda month: (0, 0, 0)
    cumulative, keep, send = pl.pallas_call(
        functools.partial(apply_kernel, orders),
        grid=(months,),
        out_shape=(
            shape(transition.shape, f32),
            shape((cohorts // 2, months, rows, states), f32),
            shape((cohorts // 2, months, rows, states), f32),
        ),
        in_specs=[
            pl.BlockSpec((1, groups) + block, by_month),
            pl.BlockSpec((1, groups) + block, by_month),
            pl.BlockSpec((groups,) + block, whole),
            SMEM,
        ],
        out_specs=(
            pl.BlockSpec((1, groups) + block, by_month),
            pl.BlockSpec(part, in_place),
            pl.BlockSpec(part, in_place),
        ),
        scratch_shapes=[pltpu.VMEM(block, f32)],
        compiler_params=params(24),
        cost_estimate=cost(6 * months * groups * square, 3 * size),
        name="apply",
    )(out_hi, out_lo, carry, share)

    for step in range(steps):
        pairs = [
            (line * cohorts + c, line * cohorts + (c ^ orders[line % 2][step]))
            for line in range(lines)
            for c in range(cohorts)
        ]
        come = lax.ppermute(send, ("tm", "cohort"), pairs)
        both = keep + come
        if step < steps - 1:
            left = both.shape[0] // 2
            keep, send = both[:left], both[left:]
    pooled = both[0]
    return cumulative, pooled


def solution(mesh):
    placed = (P("tm", "cohort", None, None), P("cohort"), P("cohort"))
    return jax.shard_map(
        functools.partial(on_device, mesh),
        mesh=mesh,
        in_specs=placed,
        out_specs=(P("tm", "cohort", None, None), P("tm", "cohort", None)),
        check_vma=False,
    )
```

```python
import functools

import jax
import jax.numpy as jnp
from jax import lax
from jax.experimental import pallas as pl
from jax.experimental.pallas import tpu as pltpu
from jax.sharding import PartitionSpec as P

kernel_weights = (1.0 / 16, 2.0 / 16, 3.0 / 16, 4.0 / 16, 3.0 / 16, 2.0 / 16, 1.0 / 16)
REACH = 3
VMEM = pl.BlockSpec(memory_space=pltpu.VMEM)
SMEM = pl.BlockSpec(memory_space=pltpu.SMEM)
ANY = pl.BlockSpec(memory_space=pl.ANY)
f32, bf16 = jnp.float32, jnp.bfloat16
shaped = jax.ShapeDtypeStruct


def split(x):
    hi = x.astype(bf16)
    return hi, (x - hi.astype(f32)).astype(bf16)


def product(a, b):
    dot = functools.partial(jnp.dot, preferred_element_type=f32)
    return dot(a[0], b[0]) + (dot(a[0], b[1]) + dot(a[1], b[0]))


def put(pair, hi_ref, lo_ref, at):
    hi_ref[at], lo_ref[at] = pair


def unit_rows(rows, states, start):
    row = lax.broadcasted_iota(jnp.int32, (rows, states), 0) + start
    return (row == lax.broadcasted_iota(jnp.int32, (rows, states), 1)).astype(f32)


def inverse_weight(month, months_all):
    value = jnp.float32(1.0)
    for edge in range(months_all):
        inside = [
            kernel_weights[k + REACH]
            for k in range(-REACH, REACH + 1)
            if 0 <= edge + k < months_all
        ]
        if len(inside) < len(kernel_weights):
            value = jnp.where(month == edge, jnp.float32(1.0 / sum(inside)), value)
    return value


def sides(months, odd):
    wait = range(months - REACH, months) if odd else range(REACH)
    return list(wait), [month for month in range(months) if month not in wait]


def outer_taps(months, odd, month):
    taps = []
    for offset in range(-REACH, REACH + 1):
        at = month + offset
        if odd and at >= months:
            taps.append((kernel_weights[offset + REACH], at - months))
        if not odd and at < 0:
            taps.append((kernel_weights[offset + REACH], at + REACH))
    return taps


def early_kernel(months_all, *refs):
    raw_ref, inner_ref, entry_ref = refs[:3]
    months, groups, states = raw_ref.shape[:3]
    open_refs, hi_refs, lo_refs = (refs[3 + k * groups : 3 + (k + 1) * groups] for k in range(3))
    total_ref, done_hi, done_lo = refs[3 + 3 * groups :]
    line = lax.axis_index("tm")
    first = line * months
    step = 32

    def finished(value, month, group, start):
        value = value * inverse_weight(first + month, months_all)
        unit = unit_rows(value.shape[0], states, start)
        return jnp.where(first + month >= entry_ref[group], value, unit)

    def run(odd):
        wait, done = sides(months, odd)
        for group in range(groups):

            @pl.loop(0, states // step)
            def _(chunk):
                start = pl.multiple_of(chunk * step, step)
                rows = pl.ds(start, step)
                own = [raw_ref[month, group, rows] for month in range(months)]
                near = [inner_ref[k, group, rows] for k in range(REACH)]
                line_up = near + own if odd else own + near
                base = REACH if odd else 0
                for month in range(months):
                    value = None
                    for offset in range(-REACH, REACH + 1):
                        at = base + month + offset
                        if 0 <= at < len(line_up):
                            term = kernel_weights[offset + REACH] * line_up[at]
                            value = term if value is None else value + term
                    if month in wait:
                        open_refs[group][wait.index(month), rows] = value
                    else:
                        at = done.index(month)
                        pair = split(finished(value, month, group, start))
                        done_hi[at, group, rows], done_lo[at, group, rows] = pair

        last = [(done_hi[0, group], done_lo[0, group]) for group in range(groups)]
        for group in range(groups):
            put(last[group], hi_refs[group], lo_refs[group], 0)
        for at in range(1, len(done)):
            for group in range(groups):
                month = (done_hi[at, group], done_lo[at, group])
                last[group] = split(product(last[group], month))
                put(last[group], hi_refs[group], lo_refs[group], at)
        return wait, last

    @pl.when(line % 2 == 0)
    def _():
        wait, last = run(False)

        @pl.when(line == 0)
        def _():
            for group in range(groups):
                parts = [
                    split(finished(open_refs[group][k], month, group, 0))
                    for k, month in enumerate(wait)
                ]
                head = parts[0]
                for part in parts[1:]:
                    head = split(product(head, part))
                tail = (hi_refs[group][months - REACH - 1],
                        lo_refs[group][months - REACH - 1])
                total_ref[group] = product(head, tail)

    @pl.when(line % 2 == 1)
    def _():
        run(True)


def lead_kernel(*refs):
    before_ref = refs[0]
    groups = before_ref.shape[0]
    hi_refs, lo_refs, out_hi, out_lo = (refs[1 + k * groups : 1 + (k + 1) * groups] for k in range(4))
    second = lax.axis_index("tm") == 1

    @pl.when(second)
    def _():
        before = [split(before_ref[group]) for group in range(groups)]
        for at in range(hi_refs[0].shape[0]):
            for group in range(groups):
                month = (hi_refs[group][at], lo_refs[group][at])
                put(split(product(before[group], month)), out_hi[group], out_lo[group], at)

    @pl.when(jnp.logical_not(second))
    def _():
        for group in range(groups):
            out_hi[group][...] = hi_refs[group][...]
            out_lo[group][...] = lo_refs[group][...]


def close_kernel(months_all, group, open_ref, outer_ref, run_hi, run_lo, entry_ref, hi_ref, lo_ref, total_ref):
    months, states = hi_ref.shape[:2]
    line = lax.axis_index("tm")
    first = line * months

    def closed(odd):
        parts = []
        for k, month in enumerate(sides(months, odd)[0]):
            value = open_ref[k]
            for weight, at in outer_taps(months, odd, month):
                value = value + weight * outer_ref[at, 0]
            value = value * inverse_weight(first + month, months_all)
            value = jnp.where(first + month >= entry_ref[group], value, unit_rows(states, states, 0))
            parts.append(split(value))
        return parts

    @pl.when(line % 2 == 0)
    def _():
        parts = closed(False)
        last = parts[0]
        put(last, hi_ref, lo_ref, 0)
        for at in range(1, REACH):
            last = split(product(last, parts[at]))
            put(last, hi_ref, lo_ref, at)
        for at in reversed(range(months - REACH)):
            value = product(last, (run_hi[at], run_lo[at]))
            if at == months - REACH - 1:
                total_ref[...] = value
            put(split(value), hi_ref, lo_ref, at + REACH)

    @pl.when(line % 2 == 1)
    def _():
        parts = closed(True)
        begun = months - REACH
        last = (run_hi[begun - 1], run_lo[begun - 1])
        for at in range(REACH):
            value = product(last, parts[at])
            last = split(value)
            put(last, hi_ref, lo_ref, begun + at)
        total_ref[...] = value
        hi_ref[:begun] = run_hi[...]
        lo_ref[:begun] = run_lo[...]


def pair_kernel(carry_ref, before_ref, total_ref, out_ref):
    ahead = split(product(split(carry_ref[...]), split(before_ref[...])))
    out_ref[...] = product(ahead, split(total_ref[...]))


def place_of(order, place):
    steps = len(order)
    return sum(order[s] for s in range(steps) if place >> (steps - 1 - s) & 1)


def halving_orders(count):
    bits = [1 << s for s in range(count.bit_length() - 1)]
    other = bits[:]
    if len(bits) > 1:
        other[0], other[1] = other[1], other[0]
    return bits, other


def apply_kernel(orders, groups, start, stop, begin, *refs):
    if begin:
        firsts, seconds, befores = (refs[k * groups : (k + 1) * groups] for k in range(3))
        refs = refs[3 * groups :]
    else:
        carry_hi, carry_lo, _ = refs[:3]
        refs = refs[3:]
    hi_refs, lo_refs = refs[:groups], refs[groups : 2 * groups]
    share_ref, cum_ref, keep_ref, send_ref = refs[2 * groups : 2 * groups + 4]
    refs = refs[2 * groups + 4 :]
    if begin:
        carry_hi, carry_lo = refs[:2]
        refs = refs[2:]
    held, mix, sems = refs
    states = held.shape[2]
    line = lax.axis_index("tm")
    me = lax.axis_index("cohort")
    rows = keep_ref.shape[2]
    half = keep_ref.shape[0]

    if begin:

        @pl.when(line < 2)
        def _():
            for group in range(groups):
                put(split(unit_rows(states, states, 0)), carry_hi, carry_lo, group)

        @pl.when(jnp.logical_and(line >= 2, line % 2 == 0))
        def _():
            for group in range(groups):
                put(split(firsts[group][...]), carry_hi, carry_lo, group)

        @pl.when(jnp.logical_and(line >= 2, line % 2 == 1))
        def _():
            for group in range(groups):
                value = product(split(seconds[group][...]), split(befores[group][...]))
                put(split(value), carry_hi, carry_lo, group)

    carry = [(carry_hi[group], carry_lo[group]) for group in range(groups)]
    copies = []
    for month in range(start, stop):
        at = month - start
        mixed = None
        for group in range(groups):
            value = product(carry[group], (hi_refs[group][month], lo_refs[group][month]))
            held[at, group] = value
            term = share_ref[group] * value
            mixed = term if mixed is None else mixed + term
        mix[at] = mixed
        copy = pltpu.make_async_copy(held.at[at], cum_ref.at[month], sems.at[at])
        copy.start()
        copies.append(copy)
    for place in range(2 * half):
        away = jnp.where(line % 2 == 0, place_of(orders[0], place), place_of(orders[1], place))
        block = pl.ds(pl.multiple_of((me ^ away) * rows, 8), rows)
        out = keep_ref if place < half else send_ref
        for at in range(stop - start):
            out[place % half, at] = mix[at, block, :]
    for copy in copies:
        copy.wait()


def halve_kernel(keep_ref, come_ref, out_keep_ref, out_send_ref):
    half = out_keep_ref.shape[0]
    out_keep_ref[...] = keep_ref[:half] + come_ref[:half]
    out_send_ref[...] = keep_ref[half:] + come_ref[half:]


def end_kernel(*refs):
    *parts, out_ref = refs
    at = 0
    for keep_ref, come_ref in zip(parts[::2], parts[1::2]):
        months = keep_ref.shape[1]
        out_ref[at : at + months] = keep_ref[0] + come_ref[0]
        at += months


def call(kernel, name, out_shape, in_specs, out_specs, flops, touched, mib=24, **more):
    return pl.pallas_call(
        kernel,
        out_shape=out_shape,
        in_specs=in_specs,
        out_specs=out_specs,
        compiler_params=pltpu.CompilerParams(vmem_limit_bytes=mib << 20),
        cost_estimate=pl.CostEstimate(
            flops=int(flops), bytes_accessed=int(touched), transcendentals=0
        ),
        name=name,
        **more,
    )


def on_device(mesh, transition, entry, share):
    months, groups, states = transition.shape[:3]
    lines, cohorts = mesh.shape["tm"], mesh.shape["cohort"]
    months_all = months * lines
    block = (states, states)
    flops = 6 * states**3
    size = 4 * states**2
    line = lax.axis_index("tm")
    odd = line % 2
    rest = months - REACH

    def months_from(start, group, count):
        return lax.dynamic_slice(transition, (start, group, 0, 0), (REACH, count) + block)

    hops = [(i, i + 1) for i in range(1, lines - 1, 2)]
    cores = [(i, i + 1) for i in range(0, lines - 1, 2)]
    both_ways = lambda pairs: pairs + [(b, a) for a, b in pairs]
    outer_start = jnp.where(odd == 1, rest, 0)
    outer = [
        lax.ppermute(months_from(outer_start, group, 1), "tm", both_ways(hops))
        for group in range(groups)
    ]
    inner = lax.ppermute(months_from(rest - outer_start, 0, groups), "tm", both_ways(cores))

    halves = [shaped((rest,) + block, bf16)] * groups
    early = call(
        functools.partial(early_kernel, months_all),
        "early",
        tuple([shaped((REACH,) + block, f32)] * groups + halves + halves + [shaped((groups,) + block, f32)]),
        [VMEM, VMEM, SMEM],
        tuple([VMEM] * (3 * groups + 1)),
        flops * groups * (rest + 2),
        size * groups * 3 * months,
        scratch_shapes=[pltpu.VMEM((rest, groups) + block, bf16)] * 2,
    )(transition, inner, entry)
    opened, run_hi, run_lo = (early[k * groups : (k + 1) * groups] for k in range(3))
    ahead = lax.ppermute(early[-1], "tm", [(0, 1)])
    led = call(
        lead_kernel,
        "lead",
        tuple(halves + halves),
        [VMEM] * (1 + 2 * groups),
        tuple([VMEM] * (2 * groups)),
        flops * groups * rest,
        size * groups * rest * 2,
    )(ahead, *run_hi, *run_lo)
    run_hi, run_lo = led[:groups], led[groups:]

    hi, lo, total, before, first, second = [], [], [], [], [], []
    for group in range(groups):
        a, b, c = call(
            functools.partial(close_kernel, months_all, group),
            f"close{group}",
            (shaped((months,) + block, bf16), shaped((months,) + block, bf16), shaped(block, f32)),
            [VMEM] * 4 + [SMEM],
            (VMEM, VMEM, VMEM),
            flops * months,
            size * months * 2,
        )(opened[group], outer[group], run_hi[group], run_lo[group], entry)
        hi.append(a)
        lo.append(b)
        total.append(c)
    for group in range(groups):
        pair = total[group]
        ones, twos = None, None
        for hop, (source, target) in enumerate(hops):
            if hop:
                pair = call(
                    pair_kernel,
                    f"pair{hop}_{group}",
                    shaped(block, f32),
                    [VMEM] * 3,
                    VMEM,
                    2 * flops,
                    4 * size,
                )(twos, before[group], total[group])
            one = lax.ppermute(pair, "tm", [(source, target)])
            two = lax.ppermute(one, "tm", [(target, target + 1)])
            if hop == 0:
                before.append(lax.ppermute(total[group], "tm", cores[1:]))
                ones, twos = one, two
            else:
                here = line // 2 == hop + 1
                ones, twos = jnp.where(here, one, ones), jnp.where(here, two, twos)
        if not hops:
            ones = twos = jnp.zeros_like(pair)
            before.append(ones)
        first.append(ones)
        second.append(twos)

    orders = halving_orders(cohorts)
    steps = len(orders[0])
    rows = states // cohorts
    middle = months // 2
    chunks = [(0, middle), (middle, months)]
    cumulative, carry, sums = None, None, []
    for start, stop in chunks:
        count = stop - start
        part = shaped((cohorts // 2, count, rows, states), f32)
        begin = start == 0
        outs = [shaped(transition.shape, f32), part, part]
        specs = [ANY, VMEM, VMEM]
        if begin:
            args = (*first, *second, *before, *hi, *lo, share)
            in_specs = [VMEM] * (5 * groups) + [SMEM]
            outs += [shaped((groups,) + block, bf16)] * 2
            specs += [VMEM, VMEM]
        else:
            args = (*carry, cumulative, *hi, *lo, share)
            in_specs = [VMEM, VMEM, ANY] + [VMEM] * (2 * groups) + [SMEM]
        made = call(
            functools.partial(apply_kernel, orders, groups, start, stop, begin),
            f"apply{start}",
            tuple(outs),
            in_specs,
            tuple(specs),
            flops * groups * count,
            size * groups * count * 3,
            input_output_aliases={} if begin else {2: 0},
            scratch_shapes=[
                pltpu.VMEM((count, groups) + block, f32),
                pltpu.VMEM((count,) + block, f32),
                pltpu.SemaphoreType.DMA((count,)),
            ],
        )(*args)
        cumulative, keep, send = made[:3]
        if begin:
            carry = made[3:]
        sums.append((keep, send))

    ends = []
    for chunk, (keep, send) in enumerate(sums):
        for step in range(steps):
            pairs = [
                (at * cohorts + c, at * cohorts + (c ^ orders[at % 2][step]))
                for at in range(lines)
                for c in range(cohorts)
            ]
            come = lax.ppermute(send, ("tm", "cohort"), pairs)
            if step < steps - 1:
                part = shaped((keep.shape[0] // 2,) + keep.shape[1:], f32)
                keep, send = call(
                    halve_kernel,
                    f"halve{chunk}_{step}",
                    (part, part),
                    [VMEM, VMEM],
                    (VMEM, VMEM),
                    keep.size,
                    12 * keep.size,
                )(keep, come)
        ends += [keep, come]
    pooled = call(
        end_kernel,
        "end",
        shaped((months, rows, states), f32),
        [VMEM] * len(ends),
        VMEM,
        months * rows * states,
        12 * months * rows * states,
    )(*ends)
    return cumulative, pooled


def solution(mesh):
    placed = (P("tm", "cohort", None, None), P("cohort"), P("cohort"))
    return jax.shard_map(
        functools.partial(on_device, mesh),
        mesh=mesh,
        in_specs=placed,
        out_specs=(P("tm", "cohort", None, None), P("tm", "cohort", None)),
        check_vma=False,
    )
```

```python
import functools

import jax
import jax.numpy as jnp
from jax import lax
from jax.experimental import pallas as pl
from jax.experimental.pallas import tpu as pltpu
from jax.sharding import PartitionSpec as P


kernel_weights = (1.0 / 16, 2.0 / 16, 3.0 / 16, 4.0 / 16, 3.0 / 16, 2.0 / 16, 1.0 / 16)
REACH = 3
VMEM = pl.BlockSpec(memory_space=pltpu.VMEM)
SMEM = pl.BlockSpec(memory_space=pltpu.SMEM)
ANY = pl.BlockSpec(memory_space=pl.ANY)
HBM = pl.BlockSpec(memory_space=pltpu.HBM)
f32, bf16 = jnp.float32, jnp.bfloat16
shaped = jax.ShapeDtypeStruct


def split(x):
    hi = x.astype(bf16)
    return hi, (x - hi.astype(f32)).astype(bf16)


def product(a, b):
    dot = functools.partial(jnp.dot, preferred_element_type=f32)
    return dot(a[0], b[0]) + (dot(a[0], b[1]) + dot(a[1], b[0]))


def put(pair, hi_ref, lo_ref, at):
    hi_ref[at], lo_ref[at] = pair


def unit_rows(rows, states, start):
    row = lax.broadcasted_iota(jnp.int32, (rows, states), 0) + start
    return (row == lax.broadcasted_iota(jnp.int32, (rows, states), 1)).astype(f32)


def inverse_weight(month, months_all):
    value = jnp.float32(1.0)
    for edge in range(months_all):
        inside = [
            kernel_weights[k + REACH]
            for k in range(-REACH, REACH + 1)
            if 0 <= edge + k < months_all
        ]
        if len(inside) < len(kernel_weights):
            value = jnp.where(month == edge, jnp.float32(1.0 / sum(inside)), value)
    return value


def sides(months, odd):
    wait = range(months - REACH, months) if odd else range(REACH)
    return list(wait), [month for month in range(months) if month not in wait]


def outer_taps(months, odd, month):
    taps = []
    for offset in range(-REACH, REACH + 1):
        at = month + offset
        if odd and at >= months:
            taps.append((kernel_weights[offset + REACH], at - months))
        if not odd and at < 0:
            taps.append((kernel_weights[offset + REACH], at + REACH))
    return taps


def cut_kernel(outside, group, raw_ref, out_ref, sem):
    late = (lax.axis_index("tm") % 2 == 1) == outside
    start = jnp.where(late, raw_ref.shape[0] - REACH, 0)
    source = raw_ref.at[pl.ds(start, REACH), pl.ds(group, out_ref.shape[1])]
    copy = pltpu.make_async_copy(source, out_ref, sem)
    copy.start()
    copy.wait()


def early_kernel(months_all, *refs):
    raw_ref, inner_ref, entry_ref, share_ref = refs[:4]
    months, groups, states = raw_ref.shape[:3]
    open_refs, hi_refs, lo_refs = (refs[4 + k * groups : 4 + (k + 1) * groups] for k in range(3))
    gate_refs = refs[4 + 3 * groups : 4 + 4 * groups]
    total_ref, part_ref, done_hi, done_lo = refs[4 + 4 * groups :]
    line = lax.axis_index("tm")
    first = line * months
    step = 32

    def finished(value, month, group, start):
        value = value * inverse_weight(first + month, months_all)
        unit = unit_rows(value.shape[0], states, start)
        return jnp.where(first + month >= entry_ref[group], value, unit)

    def run(odd):
        wait, done = sides(months, odd)
        for group in range(groups):
            part_ref[group] = jnp.full((8, states), share_ref[group], f32)
            for k, month in enumerate(wait):
                gate = inverse_weight(first + month, months_all)
                gate = jnp.where(first + month >= entry_ref[group], gate, jnp.float32(0.0))
                gate_refs[group][k] = jnp.full((8, states), gate, f32)

            @pl.loop(0, states // step)
            def _(chunk):
                start = pl.multiple_of(chunk * step, step)
                rows = pl.ds(start, step)
                own = [raw_ref[month, group, rows] for month in range(months)]
                near = [inner_ref[k, group, rows] for k in range(REACH)]
                line_up = near + own if odd else own + near
                base = REACH if odd else 0
                for month in range(months):
                    value = None
                    for offset in range(-REACH, REACH + 1):
                        at = base + month + offset
                        if 0 <= at < len(line_up):
                            term = kernel_weights[offset + REACH] * line_up[at]
                            value = term if value is None else value + term
                    if month in wait:
                        open_refs[group][wait.index(month), rows] = value
                    else:
                        at = done.index(month)
                        pair = split(finished(value, month, group, start))
                        done_hi[at, group, rows], done_lo[at, group, rows] = pair

        last = [(done_hi[0, group], done_lo[0, group]) for group in range(groups)]
        for group in range(groups):
            put(last[group], hi_refs[group], lo_refs[group], 0)
        for at in range(1, len(done)):
            for group in range(groups):
                month = (done_hi[at, group], done_lo[at, group])
                last[group] = split(product(last[group], month))
                put(last[group], hi_refs[group], lo_refs[group], at)
        return wait, last

    @pl.when(line % 2 == 0)
    def _():
        wait, _ = run(False)

        @pl.when(line == 0)
        def _():
            for group in range(groups):
                parts = [
                    split(finished(open_refs[group][k], month, group, 0))
                    for k, month in enumerate(wait)
                ]
                head = parts[0]
                for part in parts[1:]:
                    head = split(product(head, part))
                tail = (hi_refs[group][months - REACH - 1],
                        lo_refs[group][months - REACH - 1])
                total_ref[group] = product(head, tail)

    @pl.when(line % 2 == 1)
    def _():
        run(True)


def lead_kernel(*refs):
    before_ref = refs[0]
    groups = before_ref.shape[0]
    hi_refs, lo_refs, out_hi, out_lo = (refs[1 + k * groups : 1 + (k + 1) * groups] for k in range(4))
    second = lax.axis_index("tm") == 1

    @pl.when(second)
    def _():
        before = [split(before_ref[group]) for group in range(groups)]
        for at in range(hi_refs[0].shape[0]):
            for group in range(groups):
                month = (hi_refs[group][at], lo_refs[group][at])
                put(split(product(before[group], month)), out_hi[group], out_lo[group], at)

    @pl.when(jnp.logical_not(second))
    def _():
        for group in range(groups):
            out_hi[group][...] = hi_refs[group][...]
            out_lo[group][...] = lo_refs[group][...]


def closed(odd, open_ref, outer_ref, gate_ref, months):
    states = open_ref.shape[1]
    unit = unit_rows(states, states, 0)
    parts = []
    for k, month in enumerate(sides(months, odd)[0]):
        value = open_ref[k]
        for weight, at in outer_taps(months, odd, month):
            value = value + weight * outer_ref[at, 0]
        gate = gate_ref[k, 0:1, :]
        parts.append(split(jnp.where(gate > 0.0, value * gate, unit)))
    return parts


def close_odd_kernel(open_ref, outer_ref, run_hi, run_lo, gate_ref, hi_ref, lo_ref, total_ref):
    months = hi_ref.shape[0]
    begun = months - REACH

    @pl.when(lax.axis_index("tm") % 2 == 1)
    def _():
        parts = closed(True, open_ref, outer_ref, gate_ref, months)
        last = (run_hi[begun - 1], run_lo[begun - 1])
        for at in range(REACH):
            value = product(last, parts[at])
            last = split(value)
            put(last, hi_ref, lo_ref, begun + at)
        total_ref[...] = value


def close_even_kernel(open_ref, outer_ref, run_hi, run_lo, gate_ref, _hi, _lo, hi_ref, lo_ref):
    months = hi_ref.shape[0]
    begun = months - REACH

    @pl.when(lax.axis_index("tm") % 2 == 0)
    def _():
        parts = closed(False, open_ref, outer_ref, gate_ref, months)
        last = parts[0]
        put(last, hi_ref, lo_ref, 0)
        for at in range(1, REACH):
            last = split(product(last, parts[at]))
            put(last, hi_ref, lo_ref, at)
        for at in reversed(range(begun)):
            value = product(last, (run_hi[at], run_lo[at]))
            put(split(value), hi_ref, lo_ref, at + REACH)

    @pl.when(lax.axis_index("tm") % 2 == 1)
    def _():
        hi_ref[:begun] = run_hi[...]
        lo_ref[:begun] = run_lo[...]


def cross_kernel(carry_ref, hi_ref, lo_ref, out_ref):
    last = hi_ref.shape[0] - 1
    out_ref[...] = product(split(carry_ref[...]), (hi_ref[last], lo_ref[last]))


def place_of(order, place):
    steps = len(order)
    return sum(order[s] for s in range(steps) if place >> (steps - 1 - s) & 1)


def halving_orders(count):
    bits = [1 << s for s in range(count.bit_length() - 1)]
    other = bits[:]
    if len(bits) > 1:
        other[0], other[1] = other[1], other[0]
    return bits, other


def apply_kernel(orders, groups, start, begin, *refs):
    if begin:
        firsts, seconds = refs[:groups], refs[groups : 2 * groups]
        refs = refs[2 * groups :]
    else:
        carry_hi, carry_lo = refs[:2]
        refs = refs[2:]
    hi_refs, lo_refs = refs[:groups], refs[groups : 2 * groups]
    share_ref, cum_ref, keep_ref, send_ref = refs[2 * groups : 2 * groups + 4]
    refs = refs[2 * groups + 4 :]
    if begin:
        carry_hi, carry_lo = refs[:2]
        refs = refs[2:]
    (mix,) = refs
    months, _, states = cum_ref.shape[:3]
    line = lax.axis_index("tm")
    me = lax.axis_index("cohort")
    rows = keep_ref.shape[2]
    half = keep_ref.shape[0]

    if begin:

        @pl.when(line < 2)
        def _():
            for group in range(groups):
                put(split(unit_rows(states, states, 0)), carry_hi, carry_lo, group)

        @pl.when(jnp.logical_and(line >= 2, line % 2 == 0))
        def _():
            for group in range(groups):
                put(split(firsts[group][...]), carry_hi, carry_lo, group)

        @pl.when(jnp.logical_and(line >= 2, line % 2 == 1))
        def _():
            for group in range(groups):
                put(split(seconds[group][...]), carry_hi, carry_lo, group)

    carry = [(carry_hi[group], carry_lo[group]) for group in range(groups)]
    for at in range(months):
        mixed = None
        for group in range(groups):
            month = (hi_refs[group][start + at], lo_refs[group][start + at])
            value = product(carry[group], month)
            cum_ref[at, group] = value
            term = share_ref[group, 0:1, :] * value
            mixed = term if mixed is None else mixed + term
        mix[at] = mixed
    for place in range(2 * half):
        away = jnp.where(line % 2 == 0, place_of(orders[0], place), place_of(orders[1], place))
        block = pl.ds(pl.multiple_of((me ^ away) * rows, 8), rows)
        out = keep_ref if place < half else send_ref
        for at in range(months):
            out[place % half, at] = mix[at, block, :]


def store_kernel(*refs):
    *parts, out_ref, sems = refs
    copies, at = [], 0
    for k, part in enumerate(parts):
        months = part.shape[0]
        copies.append(pltpu.make_async_copy(part, out_ref.at[pl.ds(at, months)], sems.at[k]))
        at += months
    for copy in copies:
        copy.start()
    for copy in copies:
        copy.wait()


def halve_kernel(keep_ref, come_ref, out_keep_ref, out_send_ref):
    half = out_keep_ref.shape[0]
    out_keep_ref[...] = keep_ref[:half] + come_ref[:half]
    out_send_ref[...] = keep_ref[half:] + come_ref[half:]


def end_kernel(*refs):
    *parts, out_ref = refs
    at = 0
    for keep_ref, come_ref in zip(parts[::2], parts[1::2]):
        months = keep_ref.shape[1]
        out_ref[at : at + months] = keep_ref[0] + come_ref[0]
        at += months


def call(kernel, out_shape, in_specs, out_specs, flops, touched, mib=24, **more):
    def run(*args):
        return pl.pallas_call(
            kernel,
            out_shape=out_shape,
            in_specs=in_specs,
            out_specs=out_specs,
            compiler_params=pltpu.CompilerParams(vmem_limit_bytes=mib << 20),
            cost_estimate=pl.CostEstimate(
                flops=int(flops), bytes_accessed=int(touched), transcendentals=0
            ),
            **more,
        )(*args)

    return run


def month_chunks(months):
    counts = [months * 3 // 8, months * 3 // 8, months - 2 * (months * 3 // 8)]
    ends = [sum(counts[: k + 1]) for k in range(len(counts))]
    return [(end - count, end) for end, count in zip(ends, counts)]


def on_device(mesh, transition, entry, share):
    return pipeline(mesh, transition, entry, share)


def pipeline(mesh, transition, entry, share):
    source = pltpu.with_memory_space_constraint(transition, pltpu.HBM)
    months, groups, states = transition.shape[:3]
    lines, cohorts = mesh.shape["tm"], mesh.shape["cohort"]
    months_all = months * lines
    block = (states, states)
    flops = 6 * states**3
    size = 4 * states**2
    line = lax.axis_index("tm")
    rest = months - REACH

    def cut(outside, group, count):
        return call(
            functools.partial(cut_kernel, outside, group),
            shaped((REACH, count) + block, f32),
            [HBM],
            VMEM,
            0,
            2 * REACH * count * size,
            scratch_shapes=[pltpu.SemaphoreType.DMA],
        )(source)

    hops = [(i, i + 1) for i in range(1, lines - 1, 2)]
    cores = [(i, i + 1) for i in range(0, lines - 1, 2)]
    both_ways = lambda pairs: pairs + [(b, a) for a, b in pairs]
    outer = []
    for group in range(groups):
        piece = cut(True, group, 1)
        if True:
            both = lax.ppermute(piece, "tm", both_ways(hops))
            outer.append((both, both))
        else:
            down = lax.ppermute(piece, "tm", [(b, a) for a, b in hops])
            outer.append((down, lax.ppermute(piece, "tm", hops)))
    inner = lax.ppermute(cut(False, 0, groups), "tm", both_ways(cores))

    halves = [shaped((rest,) + block, bf16)] * groups
    early = call(
        functools.partial(early_kernel, months_all),
        tuple(
            [shaped((REACH,) + block, f32)] * groups
            + halves
            + halves
            + [shaped((REACH, 8, states), f32)] * groups
            + [shaped((groups,) + block, f32), shaped((groups, 8, states), f32)]
        ),
        [VMEM, VMEM, SMEM, SMEM],
        tuple([VMEM] * (4 * groups + 2)),
        flops * groups * (rest + 2),
        size * groups * 3 * months,
        scratch_shapes=[pltpu.VMEM((rest, groups) + block, bf16)] * 2,
    )(transition, inner, entry, share)
    opened, run_hi, run_lo, gates = (early[k * groups : (k + 1) * groups] for k in range(4))
    first_total, parts = early[4 * groups :]
    ahead = lax.ppermute(first_total, "tm", [(0, 1)])
    led = call(
        lead_kernel,
        tuple(halves + halves),
        [VMEM] * (1 + 2 * groups),
        tuple([VMEM] * (2 * groups)),
        flops * groups * rest,
        size * groups * rest * 2,
    )(ahead, *run_hi, *run_lo)
    run_hi, run_lo = led[:groups], led[groups:]

    all_months = shaped((months,) + block, bf16)
    hi, lo, first, second = [], [], [], []
    for group in range(groups):
        given = (run_hi[group], run_lo[group], gates[group])
        odd_hi, odd_lo, handed = call(
            close_odd_kernel,
            (all_months, all_months, shaped(block, f32)),
            [VMEM] * 5,
            (VMEM, VMEM, VMEM),
            flops * REACH,
            size * months * 2,
        )(opened[group], outer[group][0], *given)
        hi_all, lo_all = call(
            close_even_kernel,
            (all_months, all_months),
            [VMEM] * 7,
            (VMEM, VMEM),
            flops * months,
            size * months * 2,
            input_output_aliases={5: 0, 6: 1},
        )(opened[group], outer[group][1], *given, odd_hi, odd_lo)
        hi.append(hi_all)
        lo.append(lo_all)
        first.append(jnp.zeros_like(handed) if not hops else None)
        second.append(first[-1])

        def cross(carry):
            return call(cross_kernel, shaped(block, f32), [VMEM] * 3, VMEM, flops, 4 * size)(
                carry, hi_all, lo_all
            )

        for hop, (source, target) in enumerate(hops):
            if hop:
                handed = cross(second[-1])
            one = lax.ppermute(handed, "tm", [(source, target)])
            two = cross(one)
            two = lax.ppermute(two, "tm", [(target, target + 1)])
            if hop:
                here = line // 2 == hop + 1
                one, two = jnp.where(here, one, first[-1]), jnp.where(here, two, second[-1])
            first[-1], second[-1] = one, two

    orders = halving_orders(cohorts)
    steps = len(orders[0])
    rows = states // cohorts
    carry, cumulative, sums = None, [], []
    for chunk, (start, stop) in enumerate(month_chunks(months)):
        count = stop - start
        part = shaped((cohorts // 2, count, rows, states), f32)
        begin = chunk == 0
        outs = [shaped((count, groups) + block, f32), part, part]
        if begin:
            args = (*first, *second)
            outs += [shaped((groups,) + block, bf16)] * 2
        else:
            args = carry
        made = call(
            functools.partial(apply_kernel, orders, groups, start, begin),
            tuple(outs),
            [VMEM] * (len(args) + 2 * groups + 1),
            tuple([VMEM] * len(outs)),
            flops * groups * count,
            size * groups * count * 3,
            scratch_shapes=[pltpu.VMEM((count,) + block, f32)],
        )(*args, *hi, *lo, parts)
        cumulative.append(made[0])
        sums.append(made[1:3])
        if begin:
            carry = tuple(made[3:])
    cumulative = call(
        store_kernel,
        shaped(transition.shape, f32),
        [VMEM] * len(cumulative),
        ANY,
        0,
        2 * months * groups * size,
        scratch_shapes=[pltpu.SemaphoreType.DMA((len(cumulative),))],
    )(*cumulative)

    ends = []
    for keep, send in sums:
        for step in range(steps):
            pairs = [
                (at * cohorts + c, at * cohorts + (c ^ orders[at % 2][step]))
                for at in range(lines)
                for c in range(cohorts)
            ]
            come = lax.ppermute(send, ("tm", "cohort"), pairs)
            if step < steps - 1:
                part = shaped((keep.shape[0] // 2,) + keep.shape[1:], f32)
                keep, send = call(
                    halve_kernel,
                    (part, part),
                    [VMEM, VMEM],
                    (VMEM, VMEM),
                    keep.size,
                    12 * keep.size,
                )(keep, come)
        ends += [keep, come]
    pooled = call(
        end_kernel,
        shaped((months, rows, states), f32),
        [VMEM] * len(ends),
        VMEM,
        months * rows * states,
        12 * months * rows * states,
    )(*ends)
    return cumulative, pooled


def solution(mesh):
    placed = (P("tm", "cohort", None, None), P("cohort"), P("cohort"))
    return jax.shard_map(
        functools.partial(on_device, mesh),
        mesh=mesh,
        in_specs=placed,
        out_specs=(P("tm", "cohort", None, None), P("tm", "cohort", None)),
        check_vma=False,
    )
```

```python
import functools

import jax
import jax.numpy as jnp
from jax import lax
from jax.experimental import pallas as pl
from jax.experimental.pallas import tpu as pltpu
from jax.sharding import PartitionSpec as P


kernel_weights = (1.0 / 16, 2.0 / 16, 3.0 / 16, 4.0 / 16, 3.0 / 16, 2.0 / 16, 1.0 / 16)
REACH = 3
VMEM = pl.BlockSpec(memory_space=pltpu.VMEM)
SMEM = pl.BlockSpec(memory_space=pltpu.SMEM)
ANY = pl.BlockSpec(memory_space=pl.ANY)
HBM = pl.BlockSpec(memory_space=pltpu.HBM)
f32, bf16 = jnp.float32, jnp.bfloat16
shaped = jax.ShapeDtypeStruct


def split(x):
    hi = x.astype(bf16)
    return hi, (x - hi.astype(f32)).astype(bf16)


def product(a, b):
    dot = functools.partial(jnp.dot, preferred_element_type=f32)
    return dot(a[0], b[0]) + (dot(a[0], b[1]) + dot(a[1], b[0]))


def put(pair, hi_ref, lo_ref, at):
    hi_ref[at], lo_ref[at] = pair


def unit_rows(rows, states, start):
    row = lax.broadcasted_iota(jnp.int32, (rows, states), 0) + start
    return (row == lax.broadcasted_iota(jnp.int32, (rows, states), 1)).astype(f32)


def inverse_weight(month, months_all):
    value = jnp.float32(1.0)
    for edge in range(months_all):
        inside = [
            kernel_weights[k + REACH]
            for k in range(-REACH, REACH + 1)
            if 0 <= edge + k < months_all
        ]
        if len(inside) < len(kernel_weights):
            value = jnp.where(month == edge, jnp.float32(1.0 / sum(inside)), value)
    return value


def sides(months, odd):
    wait = range(months - REACH, months) if odd else range(REACH)
    return list(wait), [month for month in range(months) if month not in wait]


def outer_taps(months, odd, month):
    taps = []
    for offset in range(-REACH, REACH + 1):
        at = month + offset
        if odd and at >= months:
            taps.append((kernel_weights[offset + REACH], at - months))
        if not odd and at < 0:
            taps.append((kernel_weights[offset + REACH], at + REACH))
    return taps


def cut_kernel(outside, group, raw_ref, out_ref, sem):
    late = (lax.axis_index("tm") % 2 == 1) == outside
    start = jnp.where(late, raw_ref.shape[0] - REACH, 0)
    source = raw_ref.at[pl.ds(start, REACH), pl.ds(group, out_ref.shape[1])]
    copy = pltpu.make_async_copy(source, out_ref, sem)
    copy.start()
    copy.wait()


def early_kernel(months_all, *refs):
    raw_ref, inner_ref, entry_ref, share_ref = refs[:4]
    months, groups, states = raw_ref.shape[:3]
    open_refs, hi_refs, lo_refs = (refs[4 + k * groups : 4 + (k + 1) * groups] for k in range(3))
    gate_refs = refs[4 + 3 * groups : 4 + 4 * groups]
    total_ref, part_ref, done_hi, done_lo = refs[4 + 4 * groups :]
    line = lax.axis_index("tm")
    first = line * months
    step = 32

    def finished(value, month, group, start):
        value = value * inverse_weight(first + month, months_all)
        unit = unit_rows(value.shape[0], states, start)
        return jnp.where(first + month >= entry_ref[group], value, unit)

    def run(odd):
        wait, done = sides(months, odd)
        for group in range(groups):
            part_ref[group] = jnp.full((8, states), share_ref[group], f32)
            for k, month in enumerate(wait):
                gate = inverse_weight(first + month, months_all)
                gate = jnp.where(first + month >= entry_ref[group], gate, jnp.float32(0.0))
                gate_refs[group][k] = jnp.full((8, states), gate, f32)

            @pl.loop(0, states // step)
            def _(chunk):
                start = pl.multiple_of(chunk * step, step)
                rows = pl.ds(start, step)
                own = [raw_ref[month, group, rows] for month in range(months)]
                near = [inner_ref[k, group, rows] for k in range(REACH)]
                line_up = near + own if odd else own + near
                base = REACH if odd else 0
                for month in range(months):
                    value = None
                    for offset in range(-REACH, REACH + 1):
                        at = base + month + offset
                        if 0 <= at < len(line_up):
                            term = kernel_weights[offset + REACH] * line_up[at]
                            value = term if value is None else value + term
                    if month in wait:
                        open_refs[group][wait.index(month), rows] = value
                    else:
                        at = done.index(month)
                        pair = split(finished(value, month, group, start))
                        done_hi[at, group, rows], done_lo[at, group, rows] = pair

        last = [(done_hi[0, group], done_lo[0, group]) for group in range(groups)]
        for group in range(groups):
            put(last[group], hi_refs[group], lo_refs[group], 0)
        for at in range(1, len(done)):
            for group in range(groups):
                month = (done_hi[at, group], done_lo[at, group])
                last[group] = split(product(last[group], month))
                put(last[group], hi_refs[group], lo_refs[group], at)
        return wait, last

    @pl.when(line % 2 == 0)
    def _():
        wait, _ = run(False)

        @pl.when(line == 0)
        def _():
            for group in range(groups):
                parts = [
                    split(finished(open_refs[group][k], month, group, 0))
                    for k, month in enumerate(wait)
                ]
                head = parts[0]
                for part in parts[1:]:
                    head = split(product(head, part))
                tail = (hi_refs[group][months - REACH - 1],
                        lo_refs[group][months - REACH - 1])
                total_ref[group] = product(head, tail)

    @pl.when(line % 2 == 1)
    def _():
        run(True)


def lead_kernel(*refs):
    before_ref = refs[0]
    groups = before_ref.shape[0]
    hi_refs, lo_refs, out_hi, out_lo = (refs[1 + k * groups : 1 + (k + 1) * groups] for k in range(4))
    second = lax.axis_index("tm") == 1

    @pl.when(second)
    def _():
        before = [split(before_ref[group]) for group in range(groups)]
        for at in range(hi_refs[0].shape[0]):
            for group in range(groups):
                month = (hi_refs[group][at], lo_refs[group][at])
                put(split(product(before[group], month)), out_hi[group], out_lo[group], at)

    @pl.when(jnp.logical_not(second))
    def _():
        for group in range(groups):
            out_hi[group][...] = hi_refs[group][...]
            out_lo[group][...] = lo_refs[group][...]


def closed(lines, odd, open_ref, outer_ref, gate_ref, months):
    present = jnp.where(lax.axis_index("tm") == (lines - 1 if odd else 0), 0.0, 1.0).astype(f32)
    states = open_ref.shape[1]
    unit = unit_rows(states, states, 0)
    parts = []
    for k, month in enumerate(sides(months, odd)[0]):
        value = open_ref[k]
        for weight, at in outer_taps(months, odd, month):
            value = value + (weight * present) * outer_ref[at, 0]
        gate = gate_ref[k, 0:1, :]
        parts.append(split(jnp.where(gate > 0.0, value * gate, unit)))
    return parts


def close_odd_kernel(lines, open_ref, outer_ref, run_hi, run_lo, gate_ref, hi_ref, lo_ref, total_ref):
    months = hi_ref.shape[0]
    begun = months - REACH

    @pl.when(lax.axis_index("tm") % 2 == 1)
    def _():
        parts = closed(lines, True, open_ref, outer_ref, gate_ref, months)
        last = (run_hi[begun - 1], run_lo[begun - 1])
        for at in range(REACH):
            value = product(last, parts[at])
            last = split(value)
            put(last, hi_ref, lo_ref, begun + at)
        total_ref[...] = value


def close_even_kernel(lines, open_ref, outer_ref, run_hi, run_lo, gate_ref, _hi, _lo, hi_ref, lo_ref):
    months = hi_ref.shape[0]
    begun = months - REACH

    @pl.when(lax.axis_index("tm") % 2 == 0)
    def _():
        parts = closed(lines, False, open_ref, outer_ref, gate_ref, months)
        last = parts[0]
        put(last, hi_ref, lo_ref, 0)
        for at in range(1, REACH):
            last = split(product(last, parts[at]))
            put(last, hi_ref, lo_ref, at)
        for at in reversed(range(begun)):
            value = product(last, (run_hi[at], run_lo[at]))
            put(split(value), hi_ref, lo_ref, at + REACH)

    @pl.when(lax.axis_index("tm") % 2 == 1)
    def _():
        hi_ref[:begun] = run_hi[...]
        lo_ref[:begun] = run_lo[...]


def cross_kernel(carry_ref, hi_ref, lo_ref, out_ref):
    last = hi_ref.shape[0] - 1
    out_ref[...] = product(split(carry_ref[...]), (hi_ref[last], lo_ref[last]))


def place_of(order, place):
    steps = len(order)
    return sum(order[s] for s in range(steps) if place >> (steps - 1 - s) & 1)


def halving_orders(count):
    bits = [1 << s for s in range(count.bit_length() - 1)]
    other = bits[:]
    if len(bits) > 1:
        other[0], other[1] = other[1], other[0]
    return bits, other


def apply_kernel(orders, groups, start, begin, *refs):
    if begin:
        firsts, seconds = refs[:groups], refs[groups : 2 * groups]
        refs = refs[2 * groups :]
    else:
        carry_hi, carry_lo = refs[:2]
        refs = refs[2:]
    hi_refs, lo_refs = refs[:groups], refs[groups : 2 * groups]
    share_ref, cum_ref, keep_ref, send_ref = refs[2 * groups : 2 * groups + 4]
    refs = refs[2 * groups + 4 :]
    if begin:
        carry_hi, carry_lo = refs[:2]
        refs = refs[2:]
    (mix,) = refs
    months, _, states = cum_ref.shape[:3]
    line = lax.axis_index("tm")
    me = lax.axis_index("cohort")
    rows = keep_ref.shape[2]
    half = keep_ref.shape[0]

    if begin:

        @pl.when(line < 2)
        def _():
            for group in range(groups):
                put(split(unit_rows(states, states, 0)), carry_hi, carry_lo, group)

        @pl.when(jnp.logical_and(line >= 2, line % 2 == 0))
        def _():
            for group in range(groups):
                put(split(firsts[group][...]), carry_hi, carry_lo, group)

        @pl.when(jnp.logical_and(line >= 2, line % 2 == 1))
        def _():
            for group in range(groups):
                put(split(seconds[group][...]), carry_hi, carry_lo, group)

    carry = [(carry_hi[group], carry_lo[group]) for group in range(groups)]
    for at in range(months):
        mixed = None
        for group in range(groups):
            month = (hi_refs[group][start + at], lo_refs[group][start + at])
            value = product(carry[group], month)
            cum_ref[at, group] = value
            term = share_ref[group, 0:1, :] * value
            mixed = term if mixed is None else mixed + term
        mix[at] = mixed
    for place in range(2 * half):
        away = jnp.where(line % 2 == 0, place_of(orders[0], place), place_of(orders[1], place))
        block = pl.ds(pl.multiple_of((me ^ away) * rows, 8), rows)
        out = keep_ref if place < half else send_ref
        for at in range(months):
            out[place % half, at] = mix[at, block, :]


def store_kernel(*refs):
    *parts, out_ref, sems = refs
    copies, at = [], 0
    for k, part in enumerate(parts):
        months = part.shape[0]
        copies.append(pltpu.make_async_copy(part, out_ref.at[pl.ds(at, months)], sems.at[k]))
        at += months
    for copy in copies:
        copy.start()
    for copy in copies:
        copy.wait()


def halve_kernel(keep_ref, come_ref, out_keep_ref, out_send_ref):
    half = out_keep_ref.shape[0]
    out_keep_ref[...] = keep_ref[:half] + come_ref[:half]
    out_send_ref[...] = keep_ref[half:] + come_ref[half:]


def end_kernel(*refs):
    *parts, out_ref = refs
    at = 0
    for keep_ref, come_ref in zip(parts[::2], parts[1::2]):
        months = keep_ref.shape[1]
        out_ref[at : at + months] = keep_ref[0] + come_ref[0]
        at += months


def call(kernel, out_shape, in_specs, out_specs, flops, touched, mib=24, **more):
    def run(*args):
        return pl.pallas_call(
            kernel,
            out_shape=out_shape,
            in_specs=in_specs,
            out_specs=out_specs,
            compiler_params=pltpu.CompilerParams(vmem_limit_bytes=mib << 20),
            cost_estimate=pl.CostEstimate(
                flops=int(flops), bytes_accessed=int(touched), transcendentals=0
            ),
            **more,
        )(*args)

    return run


def month_chunks(months):
    counts = [months * 3 // 8, months * 3 // 8, months - 2 * (months * 3 // 8)]
    ends = [sum(counts[: k + 1]) for k in range(len(counts))]
    return [(end - count, end) for end, count in zip(ends, counts)]


def on_device(mesh, transition, entry, share):
    return pipeline(mesh, transition, entry, share)


def pipeline(mesh, transition, entry, share):
    source = pltpu.with_memory_space_constraint(transition, pltpu.HBM)
    months, groups, states = transition.shape[:3]
    lines, cohorts = mesh.shape["tm"], mesh.shape["cohort"]
    months_all = months * lines
    block = (states, states)
    flops = 6 * states**3
    size = 4 * states**2
    line = lax.axis_index("tm")
    rest = months - REACH

    def cut(outside, group, count):
        return call(
            functools.partial(cut_kernel, outside, group),
            shaped((REACH, count) + block, f32),
            [HBM],
            VMEM,
            0,
            2 * REACH * count * size,
            scratch_shapes=[pltpu.SemaphoreType.DMA],
        )(source)

    hops = [(i, i + 1) for i in range(1, lines - 1, 2)]
    cores = [(i, i + 1) for i in range(0, lines - 1, 2)]
    both_ways = lambda pairs: pairs + [(b, a) for a, b in pairs]
    swapped = both_ways(cores)
    round_trip = [(i, (i + 1) % lines) for i in range(lines)]
    apart = [
        (a * cohorts + c, b * cohorts + c) for a, b in both_ways(hops) for c in range(cohorts)
    ] + [
        (a * cohorts + c, a * cohorts + (c ^ 1)) for a in (0, lines - 1) for c in range(cohorts)
    ]
    outer = []
    for group in range(groups):
        piece = cut(True, group, 1)
        outer.append(lax.ppermute(piece, ("tm", "cohort"), apart))
    inner = lax.ppermute(cut(False, 0, groups), "tm", swapped)

    halves = [shaped((rest,) + block, bf16)] * groups
    early = call(
        functools.partial(early_kernel, months_all),
        tuple(
            [shaped((REACH,) + block, f32)] * groups
            + halves
            + halves
            + [shaped((REACH, 8, states), f32)] * groups
            + [shaped((groups,) + block, f32), shaped((groups, 8, states), f32)]
        ),
        [VMEM, VMEM, SMEM, SMEM],
        tuple([VMEM] * (4 * groups + 2)),
        flops * groups * (rest + 2),
        size * groups * 3 * months,
        scratch_shapes=[pltpu.VMEM((rest, groups) + block, bf16)] * 2,
    )(transition, inner, entry, share)
    opened, run_hi, run_lo, gates = (early[k * groups : (k + 1) * groups] for k in range(4))
    first_total, parts = early[4 * groups :]
    ahead = lax.ppermute(first_total, "tm", swapped)
    led = call(
        lead_kernel,
        tuple(halves + halves),
        [VMEM] * (1 + 2 * groups),
        tuple([VMEM] * (2 * groups)),
        flops * groups * rest,
        size * groups * rest * 2,
    )(ahead, *run_hi, *run_lo)
    run_hi, run_lo = led[:groups], led[groups:]

    all_months = shaped((months,) + block, bf16)
    hi, lo, first, second = [], [], [], []
    for group in range(groups):
        given = (run_hi[group], run_lo[group], gates[group])
        odd_hi, odd_lo, handed = call(
            functools.partial(close_odd_kernel, lines),
            (all_months, all_months, shaped(block, f32)),
            [VMEM] * 5,
            (VMEM, VMEM, VMEM),
            flops * REACH,
            size * months * 2,
        )(opened[group], outer[group], *given)
        hi_all, lo_all = call(
            functools.partial(close_even_kernel, lines),
            (all_months, all_months),
            [VMEM] * 7,
            (VMEM, VMEM),
            flops * months,
            size * months * 2,
            input_output_aliases={5: 0, 6: 1},
        )(opened[group], outer[group], *given, odd_hi, odd_lo)
        hi.append(hi_all)
        lo.append(lo_all)
        first.append(jnp.zeros_like(handed) if not hops else None)
        second.append(first[-1])

        def cross(carry):
            return call(cross_kernel, shaped(block, f32), [VMEM] * 3, VMEM, flops, 4 * size)(
                carry, hi_all, lo_all
            )

        for hop, (source, target) in enumerate(hops):
            if hop:
                handed = cross(second[-1])
            way = round_trip if group == groups - 1 else [(source, target)]
            one = lax.ppermute(handed, "tm", way)
            two = cross(one)
            two = lax.ppermute(two, "tm", swapped)
            if hop:
                here = line // 2 == hop + 1
                one, two = jnp.where(here, one, first[-1]), jnp.where(here, two, second[-1])
            first[-1], second[-1] = one, two

    orders = halving_orders(cohorts)
    steps = len(orders[0])
    rows = states // cohorts
    carry, cumulative, sums = None, [], []
    for chunk, (start, stop) in enumerate(month_chunks(months)):
        count = stop - start
        part = shaped((cohorts // 2, count, rows, states), f32)
        begin = chunk == 0
        outs = [shaped((count, groups) + block, f32), part, part]
        if begin:
            args = (*first, *second)
            outs += [shaped((groups,) + block, bf16)] * 2
        else:
            args = carry
        made = call(
            functools.partial(apply_kernel, orders, groups, start, begin),
            tuple(outs),
            [VMEM] * (len(args) + 2 * groups + 1),
            tuple([VMEM] * len(outs)),
            flops * groups * count,
            size * groups * count * 3,
            scratch_shapes=[pltpu.VMEM((count,) + block, f32)],
        )(*args, *hi, *lo, parts)
        cumulative.append(made[0])
        sums.append(made[1:3])
        if begin:
            carry = tuple(made[3:])
    cumulative = call(
        store_kernel,
        shaped(transition.shape, f32),
        [VMEM] * len(cumulative),
        ANY,
        0,
        2 * months * groups * size,
        scratch_shapes=[pltpu.SemaphoreType.DMA((len(cumulative),))],
    )(*cumulative)

    ends = []
    for keep, send in sums:
        for step in range(steps):
            pairs = [
                (at * cohorts + c, at * cohorts + (c ^ orders[at % 2][step]))
                for at in range(lines)
                for c in range(cohorts)
            ]
            come = lax.ppermute(send, ("tm", "cohort"), pairs)
            if step < steps - 1:
                part = shaped((keep.shape[0] // 2,) + keep.shape[1:], f32)
                keep, send = call(
                    halve_kernel,
                    (part, part),
                    [VMEM, VMEM],
                    (VMEM, VMEM),
                    keep.size,
                    12 * keep.size,
                )(keep, come)
        ends += [keep, come]
    pooled = call(
        end_kernel,
        shaped((months, rows, states), f32),
        [VMEM] * len(ends),
        VMEM,
        months * rows * states,
        12 * months * rows * states,
    )(*ends)
    return cumulative, pooled


def solution(mesh):
    placed = (P("tm", "cohort", None, None), P("cohort"), P("cohort"))
    return jax.shard_map(
        functools.partial(on_device, mesh),
        mesh=mesh,
        in_specs=placed,
        out_specs=(P("tm", "cohort", None, None), P("tm", "cohort", None)),
        check_vma=False,
    )
```

```python
import functools

import jax
import jax.numpy as jnp
from jax import lax
from jax.experimental import pallas as pl
from jax.experimental.pallas import tpu as pltpu
from jax.sharding import PartitionSpec as P


kernel_weights = (1.0 / 16, 2.0 / 16, 3.0 / 16, 4.0 / 16, 3.0 / 16, 2.0 / 16, 1.0 / 16)
REACH = 3
VMEM = pl.BlockSpec(memory_space=pltpu.VMEM)
SMEM = pl.BlockSpec(memory_space=pltpu.SMEM)
ANY = pl.BlockSpec(memory_space=pl.ANY)
HBM = pl.BlockSpec(memory_space=pltpu.HBM)
f32, bf16 = jnp.float32, jnp.bfloat16
shaped = jax.ShapeDtypeStruct


def split(x):
    hi = x.astype(bf16)
    return hi, (x - hi.astype(f32)).astype(bf16)


def product(a, b):
    dot = functools.partial(jnp.dot, preferred_element_type=f32)
    return dot(a[0], b[0]) + (dot(a[0], b[1]) + dot(a[1], b[0]))


def put(pair, hi_ref, lo_ref, at):
    hi_ref[at], lo_ref[at] = pair


def unit_rows(rows, states, start):
    row = lax.broadcasted_iota(jnp.int32, (rows, states), 0) + start
    return (row == lax.broadcasted_iota(jnp.int32, (rows, states), 1)).astype(f32)


def inverse_weight(month, months_all):
    value = jnp.float32(1.0)
    for edge in range(months_all):
        inside = [
            kernel_weights[k + REACH]
            for k in range(-REACH, REACH + 1)
            if 0 <= edge + k < months_all
        ]
        if len(inside) < len(kernel_weights):
            value = jnp.where(month == edge, jnp.float32(1.0 / sum(inside)), value)
    return value


def sides(months, odd):
    wait = range(months - REACH, months) if odd else range(REACH)
    return list(wait), [month for month in range(months) if month not in wait]


def outer_taps(months, odd, month):
    taps = []
    for offset in range(-REACH, REACH + 1):
        at = month + offset
        if odd and at >= months:
            taps.append((kernel_weights[offset + REACH], at - months))
        if not odd and at < 0:
            taps.append((kernel_weights[offset + REACH], at + REACH))
    return taps


def cut_kernel(outside, group, raw_ref, out_ref, sem):
    late = (lax.axis_index("tm") % 2 == 1) == outside
    start = jnp.where(late, raw_ref.shape[0] - REACH, 0)
    source = raw_ref.at[pl.ds(start, REACH), pl.ds(group, out_ref.shape[1])]
    copy = pltpu.make_async_copy(source, out_ref, sem)
    copy.start()
    copy.wait()


def early_kernel(months_all, *refs):
    raw_ref, inner_ref, entry_ref, share_ref = refs[:4]
    months, groups, states = raw_ref.shape[:3]
    open_refs, hi_refs, lo_refs = (refs[4 + k * groups : 4 + (k + 1) * groups] for k in range(3))
    gate_refs = refs[4 + 3 * groups : 4 + 4 * groups]
    total_ref, part_ref, done_hi, done_lo = refs[4 + 4 * groups :]
    line = lax.axis_index("tm")
    first = line * months
    step = 32

    def finished(value, month, group, start):
        value = value * inverse_weight(first + month, months_all)
        unit = unit_rows(value.shape[0], states, start)
        return jnp.where(first + month >= entry_ref[group], value, unit)

    def run(odd):
        wait, done = sides(months, odd)
        for group in range(groups):
            part_ref[group] = jnp.full((8, states), share_ref[group], f32)
            for k, month in enumerate(wait):
                gate = inverse_weight(first + month, months_all)
                gate = jnp.where(first + month >= entry_ref[group], gate, jnp.float32(0.0))
                gate_refs[group][k] = jnp.full((8, states), gate, f32)

            @pl.loop(0, states // step)
            def _(chunk):
                start = pl.multiple_of(chunk * step, step)
                rows = pl.ds(start, step)
                own = [raw_ref[month, group, rows] for month in range(months)]
                near = [inner_ref[k, group, rows] for k in range(REACH)]
                line_up = near + own if odd else own + near
                base = REACH if odd else 0
                for month in range(months):
                    value = None
                    for offset in range(-REACH, REACH + 1):
                        at = base + month + offset
                        if 0 <= at < len(line_up):
                            term = kernel_weights[offset + REACH] * line_up[at]
                            value = term if value is None else value + term
                    if month in wait:
                        open_refs[group][wait.index(month), rows] = value
                    else:
                        at = done.index(month)
                        pair = split(finished(value, month, group, start))
                        done_hi[at, group, rows], done_lo[at, group, rows] = pair

        last = [(done_hi[0, group], done_lo[0, group]) for group in range(groups)]
        for group in range(groups):
            put(last[group], hi_refs[group], lo_refs[group], 0)
        for at in range(1, len(done)):
            for group in range(groups):
                month = (done_hi[at, group], done_lo[at, group])
                last[group] = split(product(last[group], month))
                put(last[group], hi_refs[group], lo_refs[group], at)
        return wait, last

    @pl.when(line % 2 == 0)
    def _():
        wait, _ = run(False)

        @pl.when(line == 0)
        def _():
            for group in range(groups):
                parts = [
                    split(finished(open_refs[group][k], month, group, 0))
                    for k, month in enumerate(wait)
                ]
                head = parts[0]
                for part in parts[1:]:
                    head = split(product(head, part))
                tail = (hi_refs[group][months - REACH - 1],
                        lo_refs[group][months - REACH - 1])
                total_ref[group] = product(head, tail)

    @pl.when(line % 2 == 1)
    def _():
        run(True)


def lead_kernel(*refs):
    before_ref = refs[0]
    groups = before_ref.shape[0]
    hi_refs, lo_refs, out_hi, out_lo = (refs[1 + k * groups : 1 + (k + 1) * groups] for k in range(4))
    second = lax.axis_index("tm") == 1

    @pl.when(second)
    def _():
        before = [split(before_ref[group]) for group in range(groups)]
        for at in range(hi_refs[0].shape[0]):
            for group in range(groups):
                month = (hi_refs[group][at], lo_refs[group][at])
                put(split(product(before[group], month)), out_hi[group], out_lo[group], at)

    @pl.when(jnp.logical_not(second))
    def _():
        for group in range(groups):
            out_hi[group][...] = hi_refs[group][...]
            out_lo[group][...] = lo_refs[group][...]


def closed(lines, odd, open_ref, outer_ref, gate_ref, months):
    present = jnp.where(lax.axis_index("tm") == (lines - 1 if odd else 0), 0.0, 1.0).astype(f32)
    states = open_ref.shape[1]
    unit = unit_rows(states, states, 0)
    parts = []
    for k, month in enumerate(sides(months, odd)[0]):
        value = open_ref[k]
        for weight, at in outer_taps(months, odd, month):
            value = value + (weight * present) * outer_ref[at, 0]
        gate = gate_ref[k, 0:1, :]
        parts.append(split(jnp.where(gate > 0.0, value * gate, unit)))
    return parts


def close_odd_kernel(lines, open_ref, outer_ref, run_hi, run_lo, gate_ref, hi_ref, lo_ref, total_ref):
    months = hi_ref.shape[0]
    begun = months - REACH

    @pl.when(lax.axis_index("tm") % 2 == 1)
    def _():
        parts = closed(lines, True, open_ref, outer_ref, gate_ref, months)
        last = (run_hi[begun - 1], run_lo[begun - 1])
        for at in range(REACH):
            value = product(last, parts[at])
            last = split(value)
            put(last, hi_ref, lo_ref, begun + at)
        total_ref[...] = value


def close_even_kernel(lines, open_ref, outer_ref, run_hi, run_lo, gate_ref, _hi, _lo, hi_ref, lo_ref):
    months = hi_ref.shape[0]
    begun = months - REACH

    @pl.when(lax.axis_index("tm") % 2 == 0)
    def _():
        parts = closed(lines, False, open_ref, outer_ref, gate_ref, months)
        last = parts[0]
        put(last, hi_ref, lo_ref, 0)
        for at in range(1, REACH):
            last = split(product(last, parts[at]))
            put(last, hi_ref, lo_ref, at)
        for at in reversed(range(begun)):
            value = product(last, (run_hi[at], run_lo[at]))
            put(split(value), hi_ref, lo_ref, at + REACH)

    @pl.when(lax.axis_index("tm") % 2 == 1)
    def _():
        hi_ref[:begun] = run_hi[...]
        lo_ref[:begun] = run_lo[...]


def cross_kernel(carry_ref, hi_ref, lo_ref, out_ref):
    last = hi_ref.shape[0] - 1
    out_ref[...] = product(split(carry_ref[...]), (hi_ref[last], lo_ref[last]))


def place_of(order, place):
    steps = len(order)
    return sum(order[s] for s in range(steps) if place >> (steps - 1 - s) & 1)


def halving_orders(count):
    bits = [1 << s for s in range(count.bit_length() - 1)]
    other = bits[:]
    if len(bits) > 1:
        other[0], other[1] = other[1], other[0]
    return bits, other


def taken_over(first_ref, second_ref, hi_ref, lo_ref):
    line = lax.axis_index("tm")
    states = hi_ref.shape[1]

    @pl.when(line < 2)
    def _():
        put(split(unit_rows(states, states, 0)), hi_ref, lo_ref, 0)

    if first_ref is not None:

        @pl.when(jnp.logical_and(line >= 2, line % 2 == 0))
        def _():
            put(split(first_ref[...]), hi_ref, lo_ref, 0)

    if second_ref is not None:

        @pl.when(jnp.logical_and(line >= 2, line % 2 == 1))
        def _():
            put(split(second_ref[...]), hi_ref, lo_ref, 0)


def ahead_kernel(first_ref, second_ref, hi_ref, lo_ref, cum_ref, carry_hi, carry_lo):
    taken_over(first_ref, second_ref, carry_hi, carry_lo)
    carry = (carry_hi[0], carry_lo[0])
    for month in range(cum_ref.shape[0]):
        cum_ref[month] = product(carry, (hi_ref[month], lo_ref[month]))


def apply_kernel(orders, groups, start, core, *refs):
    begin = core is not None
    given, refs = (refs[:1], refs[1:]) if begin else (refs[:2], refs[2:])
    other_refs, refs = refs[: groups - 1], refs[groups - 1 :]
    hi_ref, lo_ref, share_ref = refs[:3]
    refs = refs[3 + 5 * (core == 1) :]
    cum_ref, keep_ref, send_ref = refs[:3]
    carry_hi, carry_lo = refs[3:5] if begin else given
    mix = refs[-1]
    months = cum_ref.shape[0]
    line = lax.axis_index("tm")
    me = lax.axis_index("cohort")
    rows = keep_ref.shape[2]
    half = keep_ref.shape[0]

    def run():
        if begin:
            handed = given[0]
            taken_over(*((None, handed) if core else (handed, None)), carry_hi, carry_lo)
        carry = (carry_hi[0], carry_lo[0])
        for at in range(months):
            value = product(carry, (hi_ref[start + at], lo_ref[start + at]))
            cum_ref[at] = value
            mixed = share_ref[groups - 1, 0:1, :] * value
            for group, other in enumerate(other_refs):
                mixed = mixed + share_ref[group, 0:1, :] * other[start + at]
            mix[at] = mixed
        for place in range(2 * half):
            away = [place_of(order, place) for order in orders]
            away = away[core] if begin else jnp.where(line % 2 == 0, away[0], away[1])
            block = pl.ds(pl.multiple_of((me ^ away) * rows, 8), rows)
            out = keep_ref if place < half else send_ref
            for at in range(months):
                out[place % half, at] = mix[at, block, :]

    if begin:
        pl.when(line % 2 == core)(run)
    else:
        run()


def store_kernel(*refs):
    *parts, out_ref, sems = refs
    groups = out_ref.shape[1]
    others, chunks = parts[: groups - 1], parts[groups - 1 :]
    copies, at = [], 0
    for group, part in enumerate(others):
        copies.append(pltpu.make_async_copy(part, out_ref.at[:, group], sems.at[group]))
    for k, part in enumerate(chunks):
        months = part.shape[0]
        target = out_ref.at[pl.ds(at, months), groups - 1]
        copies.append(pltpu.make_async_copy(part, target, sems.at[groups - 1 + k]))
        at += months
    for copy in copies:
        copy.start()
    for copy in copies:
        copy.wait()


def halve_kernel(keep_ref, come_ref, out_keep_ref, out_send_ref):
    half = out_keep_ref.shape[0]
    out_keep_ref[...] = keep_ref[:half] + come_ref[:half]
    out_send_ref[...] = keep_ref[half:] + come_ref[half:]


def end_kernel(*refs):
    *parts, out_ref = refs
    at = 0
    for keep_ref, come_ref in zip(parts[::2], parts[1::2]):
        months = keep_ref.shape[1]
        out_ref[at : at + months] = keep_ref[0] + come_ref[0]
        at += months


def call(kernel, out_shape, in_specs, out_specs, flops, touched, mib=24, **more):
    def run(*args):
        return pl.pallas_call(
            kernel,
            out_shape=out_shape,
            in_specs=in_specs,
            out_specs=out_specs,
            compiler_params=pltpu.CompilerParams(vmem_limit_bytes=mib << 20),
            cost_estimate=pl.CostEstimate(
                flops=int(flops), bytes_accessed=int(touched), transcendentals=0
            ),
            **more,
        )(*args)

    return run


def month_chunks(months):
    counts = [months * 3 // 8, months * 3 // 8, months - 2 * (months * 3 // 8)]
    ends = [sum(counts[: k + 1]) for k in range(len(counts))]
    return [(end - count, end) for end, count in zip(ends, counts)]


def on_device(mesh, transition, entry, share):
    return pipeline(mesh, transition, entry, share)


def pipeline(mesh, transition, entry, share):
    source = pltpu.with_memory_space_constraint(transition, pltpu.HBM)
    months, groups, states = transition.shape[:3]
    lines, cohorts = mesh.shape["tm"], mesh.shape["cohort"]
    months_all = months * lines
    block = (states, states)
    flops = 6 * states**3
    size = 4 * states**2
    line = lax.axis_index("tm")
    rest = months - REACH

    def cut(outside, group, count):
        return call(
            functools.partial(cut_kernel, outside, group),
            shaped((REACH, count) + block, f32),
            [HBM],
            VMEM,
            0,
            2 * REACH * count * size,
            scratch_shapes=[pltpu.SemaphoreType.DMA],
        )(source)

    hops = [(i, i + 1) for i in range(1, lines - 1, 2)]
    cores = [(i, i + 1) for i in range(0, lines - 1, 2)]
    both_ways = lambda pairs: pairs + [(b, a) for a, b in pairs]
    swapped = both_ways(cores)
    round_trip = [(i, (i + 1) % lines) for i in range(lines)]
    apart = [
        (a * cohorts + c, b * cohorts + c) for a, b in both_ways(hops) for c in range(cohorts)
    ] + [
        (a * cohorts + c, a * cohorts + (c ^ 1)) for a in (0, lines - 1) for c in range(cohorts)
    ]
    outer = []
    for group in range(groups):
        piece = cut(True, group, 1)
        outer.append(lax.ppermute(piece, ("tm", "cohort"), apart))
    inner = lax.ppermute(cut(False, 0, groups), "tm", swapped)

    halves = [shaped((rest,) + block, bf16)] * groups
    early = call(
        functools.partial(early_kernel, months_all),
        tuple(
            [shaped((REACH,) + block, f32)] * groups
            + halves
            + halves
            + [shaped((REACH, 8, states), f32)] * groups
            + [shaped((groups,) + block, f32), shaped((groups, 8, states), f32)]
        ),
        [VMEM, VMEM, SMEM, SMEM],
        tuple([VMEM] * (4 * groups + 2)),
        flops * groups * (rest + 2),
        size * groups * 3 * months,
        scratch_shapes=[pltpu.VMEM((rest, groups) + block, bf16)] * 2,
    )(transition, inner, entry, share)
    opened, run_hi, run_lo, gates = (early[k * groups : (k + 1) * groups] for k in range(4))
    first_total, parts = early[4 * groups :]
    ahead = lax.ppermute(first_total, "tm", swapped)
    led = call(
        lead_kernel,
        tuple(halves + halves),
        [VMEM] * (1 + 2 * groups),
        tuple([VMEM] * (2 * groups)),
        flops * groups * rest,
        size * groups * rest * 2,
    )(ahead, *run_hi, *run_lo)
    run_hi, run_lo = led[:groups], led[groups:]

    all_months = shaped((months,) + block, bf16)
    hi, lo, first, second = [], [], [], []
    for group in range(groups):
        given = (run_hi[group], run_lo[group], gates[group])
        odd_hi, odd_lo, handed = call(
            functools.partial(close_odd_kernel, lines),
            (all_months, all_months, shaped(block, f32)),
            [VMEM] * 5,
            (VMEM, VMEM, VMEM),
            flops * REACH,
            size * months * 2,
        )(opened[group], outer[group], *given)
        hi_all, lo_all = call(
            functools.partial(close_even_kernel, lines),
            (all_months, all_months),
            [VMEM] * 7,
            (VMEM, VMEM),
            flops * months,
            size * months * 2,
            input_output_aliases={5: 0, 6: 1},
        )(opened[group], outer[group], *given, odd_hi, odd_lo)
        hi.append(hi_all)
        lo.append(lo_all)
        first.append(jnp.zeros_like(handed) if not hops else None)
        second.append(first[-1])

        def cross(carry):
            return call(cross_kernel, shaped(block, f32), [VMEM] * 3, VMEM, flops, 4 * size)(
                carry, hi_all, lo_all
            )

        for hop, (source, target) in enumerate(hops):
            if hop:
                handed = cross(second[-1])
            way = round_trip if group == groups - 1 else [(source, target)]
            one = lax.ppermute(handed, "tm", way)
            two = cross(one)
            two = lax.ppermute(two, "tm", swapped)
            if hop:
                here = line // 2 == hop + 1
                one, two = jnp.where(here, one, first[-1]), jnp.where(here, two, second[-1])
            first[-1], second[-1] = one, two

    orders = halving_orders(cohorts)
    steps = len(orders[0])
    rows = states // cohorts
    others = [
        call(
            ahead_kernel,
            shaped((months,) + block, f32),
            [VMEM] * 4,
            VMEM,
            flops * months,
            3 * size * months,
            scratch_shapes=[pltpu.VMEM((1,) + block, bf16)] * 2,
        )(first[group], second[group], hi[group], lo[group])
        for group in range(groups - 1)
    ]
    known = (*others, hi[-1], lo[-1], parts)
    cumulative, sums = list(others), []
    for chunk, (start, stop) in enumerate(month_chunks(months)):
        count = stop - start
        part = shaped((cohorts // 2, count, rows, states), f32)
        outs = (shaped((count,) + block, f32), part, part)

        def apply(core, args, outs, aliases):
            return call(
                functools.partial(apply_kernel, orders, groups, start, core),
                outs,
                [VMEM] * len(args),
                tuple([VMEM] * len(outs)),
                flops * count,
                size * groups * count * 3,
                input_output_aliases=aliases,
                scratch_shapes=[pltpu.VMEM((count,) + block, f32)],
            )(*args)

        if chunk == 0:
            outs += (shaped((1,) + block, bf16),) * 2
            made = apply(0, (first[-1], *known), outs, {})
            args = (second[-1], *known, *made)
            aliases = {len(args) - 5 + k: k for k in range(5)}
            made = apply(1, args, outs, aliases)
            carry = made[3:]
        else:
            made = apply(None, (*carry, *known), outs, {})
        cumulative.append(made[0])
        sums.append(made[1:3])
    cumulative = call(
        store_kernel,
        shaped(transition.shape, f32),
        [VMEM] * len(cumulative),
        ANY,
        0,
        2 * months * groups * size,
        scratch_shapes=[pltpu.SemaphoreType.DMA((len(cumulative),))],
    )(*cumulative)

    ends = []
    for keep, send in sums:
        for step in range(steps):
            pairs = [
                (at * cohorts + c, at * cohorts + (c ^ orders[at % 2][step]))
                for at in range(lines)
                for c in range(cohorts)
            ]
            come = lax.ppermute(send, ("tm", "cohort"), pairs)
            if step < steps - 1:
                part = shaped((keep.shape[0] // 2,) + keep.shape[1:], f32)
                keep, send = call(
                    halve_kernel,
                    (part, part),
                    [VMEM, VMEM],
                    (VMEM, VMEM),
                    keep.size,
                    12 * keep.size,
                )(keep, come)
        ends += [keep, come]
    pooled = call(
        end_kernel,
        shaped((months, rows, states), f32),
        [VMEM] * len(ends),
        VMEM,
        months * rows * states,
        12 * months * rows * states,
    )(*ends)
    return cumulative, pooled


def solution(mesh):
    placed = (P("tm", "cohort", None, None), P("cohort"), P("cohort"))
    return jax.shard_map(
        functools.partial(on_device, mesh),
        mesh=mesh,
        in_specs=placed,
        out_specs=(P("tm", "cohort", None, None), P("tm", "cohort", None)),
        check_vma=False,
    )
```
